32 devices in a mesh: depth: 4 (over y, x), probe: 8 (over z, core).
Axes of the slice: x: 2, y: 2, z: 4, core: 2. Of those that a mesh axis runs over, the one named last changes fastest.
Arguments:
- probe: float32 [2, 256, 256], replicated, may hold values from -6 to 6
- phase: float32 [8, 2048, 768], P('depth', 'probe'), may hold values from -6 to 6
- row_offsets: int32 [16], P('probe'), may hold values from 0 to 2047, as said below
- col_offsets: int32 [16], P('probe'), may hold values from 0 to 512
Outputs:
- exit_waves: bfloat16 [4, 16, 2, 256, 256], P('depth', 'probe')
The draws below stay inside these ranges and needn't reach their ends.
Inputs may be any that keep to these rules, and one draw needn't show every extreme that they name: `row_offsets`: offsets 2 * i to 2 * i + 1 lie within i * 256 to (i + 1) * 256 - 1.
All inputs are finite; a program needn't handle non-finite values.
Results may differ from the reference program's by a relative error of at most 0.014.
Values may be sent and summed in bfloat16 or wider, within the bound.
No kernel may reach another device: no remote copies, remote signals or barrier semaphores. Data moves between devices by JAX's collectives and lax.ppermute only.
A program may use at most 64 MiB of HBM per device.

```python
import jax
import jax.numpy as jnp
from jax import lax

WIN = 256
STRIP = 256
OBJ_X = 768
P_DEV = 2
SL_DEV = 2
PROBES = 16
SLICES = 8
OBJ_Y = 2048
N_PROBE = 8


def edge_order(key):
    keys = jax.random.split(key, N_PROBE)
    return jax.vmap(lambda k: jax.random.permutation(k, P_DEV))(keys)


def draw_row_offsets(key, part):
    local = jax.random.randint(jax.random.fold_in(key, 11), (N_PROBE, P_DEV), 0, STRIP)
    order = edge_order(jax.random.fold_in(key, 12))
    local = jnp.where(order == 0, STRIP - 1, jnp.where(order == 1, 0, local))
    start = STRIP * jnp.arange(N_PROBE, dtype=jnp.int32)[:, None]
    return (local + start).reshape(-1).astype(jnp.int32)


def draw_col_offsets(key, part):
    local = jax.random.randint(jax.random.fold_in(key, 21), (N_PROBE, P_DEV), 0, OBJ_X - WIN + 1)
    order = edge_order(jax.random.fold_in(key, 22))
    local = jnp.where(order == 0, OBJ_X - WIN, jnp.where(order == 1, 0, local))
    return local.reshape(-1).astype(jnp.int32)


def level_of(rng, extent, shards, least, high):
    def one(position, shards_of):
        draws = jax.random.uniform(jax.random.fold_in(jax.random.fold_in(rng, 6), position), (shards_of,), jnp.float32, least / len(shards), high / len(shards))
        return jnp.repeat(jnp.exp(draws), extent[position] // shards_of).reshape((-1,) + (1,) * (len(extent) - position - 1))

    loudness = one(*shards[0])
    for cut in shards[1:]:
        loudness = loudness * one(*cut)
    return loudness


def scatter_about(own_key, dims, scale, bound, cuts=(), kind=jnp.bfloat16):
    entries = scale * jax.random.normal(own_key, dims, jnp.float32)
    if cuts:
        entries = entries * level_of(own_key, dims, cuts, -0.22, 0.18)
    return jnp.clip(entries, -bound, bound).astype(kind)


def setup_inputs(seed: int = 0) -> dict:
    seeds = jax.random.split(jax.random.key(seed), 5)
    return {
        "probe": scatter_about(seeds[0], (2, WIN, WIN), 1.0, 6.0, (), jnp.float32),
        "phase": scatter_about(seeds[1], (SLICES, OBJ_Y, OBJ_X), 1.0, 6.0, ((0, 4), (1, 8)), jnp.float32),
        "row_offsets": draw_row_offsets(jax.random.fold_in(seeds[4], 71), 0),
        "col_offsets": draw_col_offsets(jax.random.fold_in(seeds[4], 71), 0),
    }


CHIRP = 40.0


def chirp_factors(size):
    k = jnp.arange(size)
    freq = jnp.where(k < size // 2, k, k - size).astype(jnp.float32) / size
    angle = -CHIRP * freq * freq
    return lax.complex(jnp.cos(angle), jnp.sin(angle))


def reference(probe, phase, row_offsets, col_offsets):
    factor = chirp_factors(WIN)
    kernel = factor[:, None] * factor[None, :]
    incident = lax.complex(probe[0], probe[1])
    wave = jnp.broadcast_to(incident, (PROBES, WIN, WIN))
    padding = jnp.zeros((STRIP, OBJ_X), jnp.float32)
    results = []
    for group in range(SLICES // SL_DEV):
        for inner in range(SL_DEV):
            full = jnp.concatenate([phase[group * SL_DEV + inner], padding.astype(phase.dtype)], axis=0)
            windows = jax.vmap(lambda r, c: lax.dynamic_slice(full, (r.astype(jnp.int32), c.astype(jnp.int32)), (WIN, WIN)))(row_offsets, col_offsets)
            wave = wave * lax.complex(jnp.cos(windows), jnp.sin(windows))
            wave = jnp.fft.ifft2(jnp.fft.fft2(wave) * kernel)
        real_part = jnp.real(wave).astype(jnp.bfloat16)
        imag_part = jnp.imag(wave).astype(jnp.bfloat16)
        results.append(jnp.stack([real_part, imag_part], axis=1))
        real_back = lax.optimization_barrier(real_part).astype(jnp.float32)
        imag_back = lax.optimization_barrier(imag_part).astype(jnp.float32)
        wave = lax.complex(real_back, imag_back)
    return jnp.stack(results)
```

```python
import functools
import math

import numpy as np
import jax
import jax.numpy as jnp
from jax import lax
from jax.experimental import pallas as pl
from jax.experimental.pallas import tpu as pltpu
from jax.sharding import PartitionSpec as P

CHIRP = 40.0
F32 = jnp.float32
BF16 = jnp.bfloat16
OCTAVES = 120.0
ROOM = 8 * 2**20


def passed_along(block, axis, distance):
    devices = range(lax.axis_size(axis))
    route = [(i - distance, i) for i in devices if i - distance in devices]
    return lax.ppermute(block, axis, route)


def operator_tables(size):
    k = np.arange(size)
    freq = np.where(k < size // 2, k, k - size) / size
    taps = np.fft.ifft(np.exp(-1j * CHIRP * freq * freq))
    half = size // 2
    lag = (np.arange(half)[:, None] - np.arange(half)[None, :]) % size
    right, left = [], []
    for sign in (1.0, -1.0):
        part = 0.5 * (taps[lag] + sign * taps[(lag + half) % size])
        full = np.block([[part.real, part.imag], [-part.imag, part.real]]).astype(np.float32)
        high = full.astype(BF16)
        low = (full - high.astype(np.float32)).astype(BF16)
        right.append(np.concatenate([high, low], axis=0))
        left.append(np.concatenate([high.T, low.T], axis=1))
    return [jnp.asarray(np.stack(right)), jnp.asarray(np.stack(left))]


def fit(function, powers, reach):
    x = np.cos(np.pi * (np.arange(400) + 0.5) / 400) * reach
    basis = np.stack([(x / reach) ** p for p in powers], axis=1)
    found = np.linalg.lstsq(basis, function(x), rcond=None)[0]
    return [float(c / reach**p) for c, p in zip(found, powers)]


def half_angle(position):
    return position * (math.pi / OCTAVES)


SIN_FIT = fit(lambda y: math.sqrt(2.0) * np.sin(half_angle(y)), (1, 3, 5, 7), OCTAVES / 2)
COS_FIT = fit(lambda y: math.sqrt(2.0) * np.cos(half_angle(y)), (0, 2, 4, 6, 8), OCTAVES / 2)


def horner(square, coefficients):
    value = coefficients[-1]
    for c in coefficients[-2::-1]:
        value = value * square + c
    return value


def phase_factor(code):
    position = jnp.log2(code)
    square = position * position
    sine = position * horner(square, SIN_FIT)
    cosine = horner(square, COS_FIT)
    return 1.0 - sine * sine, sine * cosine


def coded(phase):
    turns = phase * (0.5 / math.pi)
    return jnp.exp2(OCTAVES * (turns - jnp.round(turns))).astype(BF16)


def window_kernel(rows_ref, cols_ref, edge_ref, own_ref, next_ref, *refs):
    outs, scratch = refs[:-1], refs[-1]
    layers, strip, width = own_ref.shape
    size = outs[0].shape[-1]
    span = size + 128
    edge = edge_ref[0].astype(F32)
    line = lax.broadcasted_iota(jnp.int32, (strip, span), 0)
    for j, out in enumerate(outs):
        r = rows_ref[j]
        c = cols_ref[j]
        base = jnp.minimum(c // 128, (width - span) // 128)
        shift = c - base * 128
        lanes = pl.ds(pl.multiple_of(base * 128, 128), span)
        for s in range(layers):
            own = own_ref[s, :, lanes].astype(F32)
            following = next_ref[s, :, lanes].astype(F32) + edge
            merged = jnp.where(line >= r, own, following)
            turned = pltpu.roll(merged, span - shift, 1)[:, :size]
            for part in range(size // 128):
                columns = turned[:, part * 128 : (part + 1) * 128]
                scratch[part, pl.ds(0, strip), :] = columns
                scratch[part, pl.ds(strip, strip), :] = columns
                out[s, :, part * 128 : (part + 1) * 128] = scratch[part, pl.ds(r, size), :].astype(BF16)


SMEM = pl.BlockSpec(memory_space=pltpu.SMEM)
VMEM = pl.BlockSpec(memory_space=pltpu.VMEM)


def windows(own, following, rows, cols, edge, size):
    layers, strip, _ = own.shape
    count = rows.shape[0]
    return pl.pallas_call(
        window_kernel,
        out_shape=[jax.ShapeDtypeStruct((layers, size, size), BF16)] * count,
        in_specs=[SMEM, SMEM, SMEM, VMEM, VMEM],
        out_specs=[VMEM] * count,
        scratch_shapes=[pltpu.VMEM((size // 128, 2 * strip, 128), F32)],
        compiler_params=pltpu.CompilerParams(vmem_limit_bytes=ROOM),
    )(rows, cols, edge, own, following)


def product(a, b):
    return jnp.dot(a, b, preferred_element_type=F32)


def propagated(real, imag, right_ref, left_ref):
    size = real.shape[-1]
    half = size // 2

    def right(k, sign):
        data = jnp.concatenate([real[:, :half] + sign * real[:, half:], imag[:, :half] + sign * imag[:, half:]], axis=1).astype(BF16)
        return product(data, right_ref[k, :size]) + product(data, right_ref[k, size:])

    plus, minus = right(0, 1.0), right(1, -1.0)
    re = jnp.concatenate([plus[:, :half], minus[:, :half]], axis=1)
    im = jnp.concatenate([plus[:, half:], minus[:, half:]], axis=1)

    def left(k, sign):
        data = jnp.concatenate([re[:half] + sign * re[half:], im[:half] + sign * im[half:]], axis=0).astype(BF16)
        return product(left_ref[k, :, :size], data) + product(left_ref[k, :, size:], data)

    top, low = left(0, 1.0), left(1, -1.0)
    re = jnp.concatenate([top[:half] + low[:half], top[:half] - low[:half]], axis=0)
    im = jnp.concatenate([top[half:] + low[half:], top[half:] - low[half:]], axis=0)
    real = jnp.concatenate([re[:, :half] + re[:, half:], re[:, :half] - re[:, half:]], axis=1)
    imag = jnp.concatenate([im[:, :half] + im[:, half:], im[:, :half] - im[:, half:]], axis=1)
    return real, imag


def group_kernel(distance, place, group_ref, probe_ref, wave_ref, layers_ref, right_ref, left_ref, *refs):
    out_ref = refs[-1]
    out = out_ref if place is None else out_ref.at[0]
    group = group_ref[0]

    @pl.when(group >= distance)
    def _():
        first = group == distance
        real = jnp.where(first, probe_ref[0], wave_ref[0].astype(F32))
        imag = jnp.where(first, probe_ref[1], wave_ref[1].astype(F32))
        for s in range(layers_ref.shape[0]):
            cosine, sine = phase_factor(layers_ref[s].astype(F32))
            real, imag = cosine * real - sine * imag, cosine * imag + sine * real
            real, imag = propagated(real, imag, right_ref, left_ref)
        out[0] = real.astype(BF16)
        out[1] = imag.astype(BF16)


def through_group(distance, group, probe, wave, layers, tables, place=None, count=None, partial=None):
    arguments = [group, probe, wave, layers, *tables]
    specs = [SMEM] + [VMEM] * 5
    aliases = {}
    if place is None:
        out_shape, out_spec = jax.ShapeDtypeStruct(wave.shape, BF16), VMEM
    else:
        out_shape = jax.ShapeDtypeStruct((count, *wave.shape), BF16)
        out_spec = pl.BlockSpec((1, *wave.shape), lambda i: (place, 0, 0, 0))
        specs = [SMEM] + [pl.BlockSpec(a.shape, lambda i, n=a.ndim: (0,) * n) for a in arguments[1:]]
        if partial is not None:
            arguments.append(partial)
            specs.append(pl.BlockSpec(memory_space=pl.ANY))
            aliases = {len(arguments) - 1: 0}
    return pl.pallas_call(
        functools.partial(group_kernel, distance, place),
        out_shape=out_shape,
        grid=() if place is None else (1,),
        in_specs=specs,
        out_specs=out_spec,
        input_output_aliases=aliases,
        compiler_params=pltpu.CompilerParams(vmem_limit_bytes=ROOM),
    )(*arguments)


def gathered(layers, groups):
    arrived = {0: layers}
    for distance in range(1, groups):
        arrived[distance] = [None] * len(layers)
    for j, block in enumerate(layers):
        for distance in range(groups - 1, 0, -1):
            arrived[distance][j] = passed_along(block, "depth", distance)
    return arrived


def body(probe, phase, row_offsets, col_offsets):
    size = probe.shape[-1]
    strip = phase.shape[1]
    count = row_offsets.shape[0]
    groups = lax.axis_size("depth")
    strips = lax.axis_size("probe")
    group = lax.axis_index("depth").astype(jnp.int32).reshape(1)
    place = lax.axis_index("probe")
    own = coded(phase)
    following = passed_along(own, "probe", -1)
    rows = row_offsets - place * strip
    edge = (place == strips - 1).astype(jnp.int32).reshape(1)
    layers = windows(own, following, rows, col_offsets, edge, size)
    tables = operator_tables(size)
    arrived = gathered(layers, groups)
    result = None
    for j in range(count):
        wave = jnp.zeros((2, size, size), BF16)
        for distance in range(groups - 1, 0, -1):
            wave = through_group(distance, group, probe, wave, arrived[distance][j], tables)
        result = through_group(0, group, probe, wave, arrived[0][j], tables, j, count, result)
    return result[None]


def solution(mesh):
    return jax.shard_map(
        body,
        mesh=mesh,
        in_specs=(P(), P("depth", "probe", None), P("probe"), P("probe")),
        out_specs=P("depth", "probe", None, None, None),
        check_vma=False,
    )
```

```python
import functools
import math

import numpy as np
import jax
import jax.numpy as jnp
from jax import lax
from jax.experimental import pallas as pl
from jax.experimental.pallas import tpu as pltpu
from jax.sharding import PartitionSpec as P


CHIRP = 40.0
F32 = jnp.float32
BF16 = jnp.bfloat16
OCTAVES = 120.0
ROOM = 8 * 2**20


def handed_down(block, parity):
    strips = lax.axis_size("probe")
    return lax.ppermute(block, "probe", [(i + 1, i) for i in range(parity, strips - 1, 2)])


def sent_on(block, parity, pairs):
    strips = lax.axis_size("probe")
    route = [(a * strips + p, b * strips + p) for a, b in pairs for p in range(parity, strips, 2)]
    return lax.ppermute(block, ("depth", "probe"), route)


def operator_tables(size):
    k = np.arange(size)
    freq = np.where(k < size // 2, k, k - size) / size
    taps = np.fft.ifft(np.exp(-1j * CHIRP * freq * freq))
    half = size // 2
    lag = (np.arange(half)[:, None] - np.arange(half)[None, :]) % size
    right, left = [], []
    for sign in (1.0, -1.0):
        part = 0.5 * (taps[lag] + sign * taps[(lag + half) % size])
        full = np.block([[part.real, part.imag], [-part.imag, part.real]]).astype(np.float32)
        high = full.astype(BF16)
        low = (full - high.astype(np.float32)).astype(BF16)
        right.append(np.concatenate([high, low], axis=0))
        left.append(np.concatenate([high.T, low.T], axis=1))
    return [jnp.asarray(np.stack(right)), jnp.asarray(np.stack(left))]


def fit(function, powers, reach):
    x = np.cos(np.pi * (np.arange(400) + 0.5) / 400) * reach
    basis = np.stack([(x / reach) ** p for p in powers], axis=1)
    found = np.linalg.lstsq(basis, function(x), rcond=None)[0]
    return [float(c / reach**p) for c, p in zip(found, powers)]


def half_angle(position):
    return position * (math.pi / OCTAVES)


SIN_FIT = fit(lambda y: math.sqrt(2.0) * np.sin(half_angle(y)), (1, 3, 5, 7), OCTAVES / 2)
COS_FIT = fit(lambda y: math.sqrt(2.0) * np.cos(half_angle(y)), (0, 2, 4, 6, 8), OCTAVES / 2)


def horner(square, coefficients):
    value = coefficients[-1]
    for c in coefficients[-2::-1]:
        value = value * square + c
    return value


def phase_factor(code):
    position = jnp.log2(code)
    square = position * position
    sine = position * horner(square, SIN_FIT)
    cosine = horner(square, COS_FIT)
    return 1.0 - sine * sine, sine * cosine


def coded(phase):
    turns = phase * (0.5 / math.pi)
    return jnp.exp2(OCTAVES * (turns - jnp.round(turns))).astype(BF16)


SMEM = pl.BlockSpec(memory_space=pltpu.SMEM)
VMEM = pl.BlockSpec(memory_space=pltpu.VMEM)


def product(a, b):
    return jnp.dot(a, b, preferred_element_type=F32)


def propagated(real, imag, right_ref, left_ref):
    size = real.shape[-1]
    half = size // 2

    def right(k, sign):
        data = jnp.concatenate([real[:, :half] + sign * real[:, half:], imag[:, :half] + sign * imag[:, half:]], axis=1).astype(BF16)
        return product(data, right_ref[k, :size]) + product(data, right_ref[k, size:])

    plus, minus = right(0, 1.0), right(1, -1.0)
    re = jnp.concatenate([plus[:, :half], minus[:, :half]], axis=1)
    im = jnp.concatenate([plus[:, half:], minus[:, half:]], axis=1)

    def left(k, sign):
        data = jnp.concatenate([re[:half] + sign * re[half:], im[:half] + sign * im[half:]], axis=0).astype(BF16)
        return product(left_ref[k, :, :size], data) + product(left_ref[k, :, size:], data)

    top, low = left(0, 1.0), left(1, -1.0)
    re = jnp.concatenate([top[:half] + low[:half], top[:half] - low[:half]], axis=0)
    im = jnp.concatenate([top[half:] + low[half:], top[half:] - low[half:]], axis=0)
    real = jnp.concatenate([re[:, :half] + re[:, half:], re[:, :half] - re[:, half:]], axis=1)
    imag = jnp.concatenate([im[:, :half] + im[:, half:], im[:, :half] - im[:, half:]], axis=1)
    return real, imag


def sliced(real, imag, code, right_ref, left_ref):
    cosine, sine = phase_factor(code.astype(F32))
    real, imag = cosine * real - sine * imag, cosine * imag + sine * real
    return propagated(real, imag, right_ref, left_ref)


def first_kernel(j, parity, where_ref, rows_ref, cols_ref, own_ref, next_ref, probe_ref, right_ref, left_ref, *refs):
    out_ref, scratch = refs[-2:]
    layers, strip, width = own_ref.shape
    size = out_ref.shape[-1]
    span = size + 128

    @pl.when(where_ref[1] % 2 == parity)
    def _():
        edge = where_ref[2].astype(F32)
        line = lax.broadcasted_iota(jnp.int32, (strip, span), 0)
        r = rows_ref[j]
        c = cols_ref[j]
        base = jnp.minimum(c // 128, (width - span) // 128)
        shift = c - base * 128
        lanes = pl.ds(pl.multiple_of(base * 128, 128), span)
        for s in range(layers):
            own = own_ref[s, :, lanes].astype(F32)
            following = next_ref[s, :, lanes].astype(F32) + edge
            merged = jnp.where(line >= r, own, following)
            turned = pltpu.roll(merged, span - shift, 1)[:, :size]
            for part in range(size // 128):
                columns = turned[:, part * 128 : (part + 1) * 128]
                scratch[part, pl.ds(0, strip), :] = columns
                scratch[part, pl.ds(strip, strip), :] = columns
                out_ref[s, :, part * 128 : (part + 1) * 128] = scratch[part, pl.ds(r, size), :].astype(BF16)

        @pl.when(where_ref[0] == 0)
        def _():
            real, imag = probe_ref[0], probe_ref[1]
            for s in range(layers):
                real, imag = sliced(real, imag, out_ref[s], right_ref, left_ref)
            out_ref[0] = real.astype(BF16)
            out_ref[1] = imag.astype(BF16)


def first_group(j, parity, where, rows, cols, own, following, probe, tables, after):
    layers, strip, _ = own.shape
    size = probe.shape[-1]
    return pl.pallas_call(
        functools.partial(first_kernel, j, parity),
        out_shape=jax.ShapeDtypeStruct((layers, size, size), BF16),
        in_specs=[SMEM, SMEM, SMEM] + [VMEM] * (5 + len(after)),
        out_specs=VMEM,
        scratch_shapes=[pltpu.VMEM((size // 128, 2 * strip, 128), F32)],
        compiler_params=pltpu.CompilerParams(vmem_limit_bytes=ROOM),
    )(where, rows, cols, own, following, probe, *tables, *after)


def chain_kernel(groups, before, where_ref, right_ref, left_ref, *refs):
    arrived = (refs[:groups], refs[groups : 2 * groups])
    out_ref, wave_ref = refs[-2], refs[-1]
    group = where_ref[0]
    parity = where_ref[1] % 2

    def block(offset, s):
        value = jnp.where(parity == 0, arrived[0][0][s], arrived[1][0][s])
        for m in range(1, groups):
            value = jnp.where(offset == m, jnp.where(parity == 0, arrived[0][m][s], arrived[1][m][s]), value)
        return value

    for s in range(2):
        wave_ref[s] = block(group, s)

    def step(g, _):
        real, imag = wave_ref[0].astype(F32), wave_ref[1].astype(F32)
        for s in range(arrived[0][0].shape[0]):
            real, imag = sliced(real, imag, block(g ^ group, s), right_ref, left_ref)
        wave_ref[0] = real.astype(BF16)
        wave_ref[1] = imag.astype(BF16)
        return 0

    lax.fori_loop(1, group + 1, step, 0)
    out_ref[before] = wave_ref[...]
    for j in range(before):
        out_ref[j] = refs[2 * groups + j][0]


def chain(where, tables, even, odd, finished):
    groups = len(even)
    shape = (2, *even[0].shape[1:])
    arguments = [where, *tables, *even, *odd, *finished]
    return pl.pallas_call(
        functools.partial(chain_kernel, groups, len(finished)),
        out_shape=jax.ShapeDtypeStruct((len(finished) + 1, *shape), BF16),
        in_specs=[SMEM] + [VMEM] * (len(arguments) - 1),
        out_specs=VMEM,
        scratch_shapes=[pltpu.VMEM(shape, BF16)],
        compiler_params=pltpu.CompilerParams(vmem_limit_bytes=ROOM),
    )(*arguments)


def mark_kernel(block_ref, out_ref):
    out_ref[...] = block_ref[0, :16, :128]


def mark(block):
    return pl.pallas_call(
        mark_kernel,
        out_shape=jax.ShapeDtypeStruct((16, 128), BF16),
        in_specs=[VMEM],
        out_specs=VMEM,
        compiler_params=pltpu.CompilerParams(vmem_limit_bytes=ROOM),
    )(block)


def body(probe, phase, row_offsets, col_offsets):
    size = probe.shape[-1]
    strip = phase.shape[1]
    count = row_offsets.shape[0]
    groups = lax.axis_size("depth")
    strips = lax.axis_size("probe")
    group = lax.axis_index("depth")
    place = lax.axis_index("probe")
    where = jnp.stack([group, place, (place == strips - 1).astype(jnp.int32)]).astype(jnp.int32)
    rows = row_offsets - place * strip
    tables = operator_tables(size)
    own = coded(phase)
    following = {}
    for parity in (1, 0):
        following[parity] = handed_down(own, parity)
    arrived = {0: [], 1: []}
    after = []
    for parity in (0, 1):
        for j in range(count):
            first = first_group(j, parity, where, rows, col_offsets, own, following[parity], probe, tables, after)
            after = [first]
            blocks = {0: first}
            for m in ORDER if groups == 4 else range(1, groups):
                blocks[m] = sent_on(first, parity, [(i, i ^ m) for i in range(groups) if i < i ^ m < groups])
            arrived[parity].append([blocks[m] for m in range(groups)])
        if parity == 0:
            after = after + [mark(first)]
    finished = []
    for j in range(count):
        wave = chain(where, tables, arrived[0][j], arrived[1][j], finished if j == count - 1 else [])
        finished.append(wave)
    return wave[None]


ORDER = (2, 3, 1)


def solution(mesh):
    return jax.shard_map(
        body,
        mesh=mesh,
        in_specs=(P(), P("depth", "probe", None), P("probe"), P("probe")),
        out_specs=P("depth", "probe", None, None, None),
        check_vma=False,
    )
```

```python
import functools
import math

import numpy as np
import jax
import jax.numpy as jnp
from jax import lax
from jax.experimental import pallas as pl
from jax.experimental.pallas import tpu as pltpu
from jax.sharding import PartitionSpec as P


CHIRP = 40.0
F32 = jnp.float32
BF16 = jnp.bfloat16
OCTAVES = 120.0
ROOM = 8 * 2**20


def handed_down(block, parity):
    strips = lax.axis_size("probe")
    return lax.ppermute(block, "probe", [(i + 1, i) for i in range(parity, strips - 1, 2)])


def sent_on(block, parities, pairs):
    strips = lax.axis_size("probe")
    route = [(a * strips + p, b * strips + p) for a, b in pairs for p in range(strips) if p % 2 in parities]
    return lax.ppermute(block, ("depth", "probe"), route)


def operator_tables(size):
    k = np.arange(size)
    freq = np.where(k < size // 2, k, k - size) / size
    taps = np.fft.ifft(np.exp(-1j * CHIRP * freq * freq))
    half = size // 2
    lag = (np.arange(half)[:, None] - np.arange(half)[None, :]) % size
    right, left = [], []
    for sign in (1.0, -1.0):
        part = 0.5 * (taps[lag] + sign * taps[(lag + half) % size])
        full = np.block([[part.real, part.imag], [-part.imag, part.real]]).astype(np.float32)
        high = full.astype(BF16)
        low = (full - high.astype(np.float32)).astype(BF16)
        right.append(np.concatenate([high, low], axis=0))
        left.append(np.concatenate([high.T, low.T], axis=1))
    return [jnp.asarray(np.stack(right)), jnp.asarray(np.stack(left))]


def fit(function, powers, reach):
    x = np.cos(np.pi * (np.arange(400) + 0.5) / 400) * reach
    basis = np.stack([(x / reach) ** p for p in powers], axis=1)
    found = np.linalg.lstsq(basis, function(x), rcond=None)[0]
    return [float(c / reach**p) for c, p in zip(found, powers)]


REACH = 0.5 * OCTAVES * math.log(2.0)


def half_angle(position):
    return position * (0.5 * math.pi / REACH)


SIN_FIT = fit(lambda y: math.sqrt(2.0) * np.sin(half_angle(y)), (1, 3, 5, 7), REACH)
COS_FIT = fit(lambda y: math.sqrt(2.0) * np.cos(half_angle(y)), (0, 2, 4, 6), REACH)


def horner(square, coefficients):
    value = coefficients[-1]
    for c in coefficients[-2::-1]:
        value = value * square + c
    return value


def phase_factor(code):
    position = jnp.log(code)
    square = position * position
    sine = position * horner(square, SIN_FIT)
    cosine = horner(square, COS_FIT)
    return 1.0 - sine * sine, sine * cosine


def coded(phase):
    turns = phase * (0.5 / math.pi)
    return jnp.exp2(OCTAVES * (turns - jnp.round(turns))).astype(BF16)


SMEM = pl.BlockSpec(memory_space=pltpu.SMEM)
VMEM = pl.BlockSpec(memory_space=pltpu.VMEM)


def product(a, b):
    return jnp.dot(a, b, preferred_element_type=F32)


def propagated(real, imag, right_ref, left_ref):
    size = real.shape[-1]
    half = size // 2

    def right(k, combine):
        data = jnp.concatenate([combine(real[:, :half], real[:, half:]), combine(imag[:, :half], imag[:, half:])], axis=1).astype(BF16)
        return product(data, right_ref[k, :size]) + product(data, right_ref[k, size:])

    plus, minus = right(0, jnp.add), right(1, jnp.subtract)
    re = jnp.concatenate([plus[:, :half], minus[:, :half]], axis=1)
    im = jnp.concatenate([plus[:, half:], minus[:, half:]], axis=1)

    def left(k, combine):
        data = jnp.concatenate([combine(re[:half], re[half:]), combine(im[:half], im[half:])], axis=0).astype(BF16)
        return product(left_ref[k, :, :size], data) + product(left_ref[k, :, size:], data)

    top, low = left(0, jnp.add), left(1, jnp.subtract)
    re = jnp.concatenate([top[:half] + low[:half], top[:half] - low[:half]], axis=0)
    im = jnp.concatenate([top[half:] + low[half:], top[half:] - low[half:]], axis=0)
    real = jnp.concatenate([re[:, :half] + re[:, half:], re[:, :half] - re[:, half:]], axis=1)
    imag = jnp.concatenate([im[:, :half] + im[:, half:], im[:, :half] - im[:, half:]], axis=1)
    return real, imag


def sliced(real, imag, code, right_ref, left_ref):
    cosine, sine = phase_factor(code.astype(F32))
    real, imag = cosine * real - sine * imag, cosine * imag + sine * real
    return propagated(real, imag, right_ref, left_ref)


def first_kernel(count, parity, starts_ref, own_ref, next_ref, probe_ref, right_ref, left_ref, *refs):
    outs, scratch = refs[-1 - count : -1], refs[-1]
    layers, strip, width = own_ref.shape
    size = outs[0].shape[-1]
    span = size + 128
    place = lax.axis_index("probe")

    @pl.when(place % 2 == parity)
    def _():
        edge = (place == lax.axis_size("probe") - 1).astype(F32)
        line = lax.broadcasted_iota(jnp.int32, (strip, span), 0)
        for j, out in enumerate(outs):
            r = starts_ref[j, 0]
            c = starts_ref[j, 1]
            base = jnp.minimum(c // 128, (width - span) // 128)
            shift = c - base * 128
            lanes = pl.ds(pl.multiple_of(base * 128, 128), span)
            for s in range(layers):
                own = own_ref[s, :, lanes].astype(F32)
                following = next_ref[s, :, lanes].astype(F32) + edge
                merged = jnp.where(line >= r, own, following)
                turned = pltpu.roll(merged, span - shift, 1)[:, :size]
                for part in range(size // 128):
                    columns = turned[:, part * 128 : (part + 1) * 128]
                    scratch[part, pl.ds(0, strip), :] = columns
                    scratch[part, pl.ds(strip, strip), :] = columns
                    out[s, :, part * 128 : (part + 1) * 128] = scratch[part, pl.ds(r, size), :].astype(BF16)

        @pl.when(lax.axis_index("depth") == 0)
        def _():
            waves = [(probe_ref[0], probe_ref[1])] * count
            for s in range(layers):
                waves = [sliced(*wave, out[s], right_ref, left_ref) for wave, out in zip(waves, outs)]
            for (real, imag), out in zip(waves, outs):
                out[0] = real.astype(BF16)
                out[1] = imag.astype(BF16)


def first_group(parity, starts, own, following, probe, tables, after):
    layers, strip, _ = own.shape
    size = probe.shape[-1]
    count = starts.shape[0]
    return pl.pallas_call(
        functools.partial(first_kernel, count, parity),
        out_shape=[jax.ShapeDtypeStruct((layers, size, size), BF16)] * count,
        in_specs=[SMEM] + [VMEM] * (5 + len(after)),
        out_specs=[VMEM] * count,
        scratch_shapes=[pltpu.VMEM((size // 128, 2 * strip, 128), F32)],
        compiler_params=pltpu.CompilerParams(vmem_limit_bytes=ROOM),
    )(starts, own, following, probe, *tables, *after)


def through_groups(wave_ref, first, groups, block, layers, right_ref, left_ref):
    group = lax.axis_index("depth")
    for g in range(first, groups):

        @pl.when(g <= group)
        def _():
            real, imag = wave_ref[0].astype(F32), wave_ref[1].astype(F32)
            for s in range(layers):
                real, imag = sliced(real, imag, block(g, s), right_ref, left_ref)
            wave_ref[0] = real.astype(BF16)
            wave_ref[1] = imag.astype(BF16)


def chain_kernel(groups, distances, before, starting, right_ref, left_ref, *refs):
    some = len(distances)
    arrived = tuple(dict(zip(distances, refs[k * some : (k + 1) * some])) for k in range(2))
    more = refs[2 * some :]
    out_ref, wave_ref = refs[-2], refs[-1]
    group = lax.axis_index("depth")
    even = lax.axis_index("probe") % 2 == 0

    def block(g, s):
        value = None
        for m in sorted({g ^ own for own in range(g, groups)}):
            this = jnp.where(even, arrived[0][m][s], arrived[1][m][s])
            value = this if value is None else jnp.where(group ^ g == m, this, value)
        return value

    for s in range(2):
        if starting:
            value = jnp.where(even, arrived[0][0][s], arrived[1][0][s])
            for k in range(starting):
                value = jnp.where(group == k + 1, more[k][s], value)
            wave_ref[s] = value
        else:
            wave_ref[s] = block(0, s)
    through_groups(wave_ref, 2 if starting else 1, groups, block, arrived[0][0].shape[0], right_ref, left_ref)
    out_ref[before] = wave_ref[...]
    for j in range(before):
        out_ref[j] = more[starting + j][0]


def chain(groups, tables, even, odd, starting, finished):
    distances = sorted(even)
    shape = (2, *even[0].shape[1:])
    arguments = [*tables, *(even[m] for m in distances), *(odd[m] for m in distances), *starting, *finished]
    return pl.pallas_call(
        functools.partial(chain_kernel, groups, distances, len(finished), len(starting)),
        out_shape=jax.ShapeDtypeStruct((len(finished) + 1, *shape), BF16),
        in_specs=[VMEM] * len(arguments),
        out_specs=VMEM,
        scratch_shapes=[pltpu.VMEM(shape, BF16)],
        compiler_params=pltpu.CompilerParams(vmem_limit_bytes=ROOM),
    )(*arguments)


def second_kernel(right_ref, left_ref, even_own_ref, even_near_ref, odd_own_ref, odd_near_ref, out_ref):
    even = lax.axis_index("probe") % 2 == 0

    @pl.when(lax.axis_index("depth") == 1)
    def _():
        real, imag = [jnp.where(even, even_near_ref[s], odd_near_ref[s]).astype(F32) for s in range(2)]
        for s in range(even_own_ref.shape[0]):
            real, imag = sliced(real, imag, jnp.where(even, even_own_ref[s], odd_own_ref[s]), right_ref, left_ref)
        out_ref[0] = real.astype(BF16)
        out_ref[1] = imag.astype(BF16)


def second_group(tables, even, odd):
    arguments = [*tables, even[0], even[1], odd[0], odd[1]]
    return pl.pallas_call(
        second_kernel,
        out_shape=jax.ShapeDtypeStruct((2, *even[0].shape[1:]), BF16),
        in_specs=[VMEM] * len(arguments),
        out_specs=VMEM,
        compiler_params=pltpu.CompilerParams(vmem_limit_bytes=ROOM),
    )(*arguments)


def mark_kernel(block_ref, out_ref):
    out_ref[...] = block_ref[0, :16, :128]


def mark(block):
    return pl.pallas_call(
        mark_kernel,
        out_shape=jax.ShapeDtypeStruct((16, 128), BF16),
        in_specs=[VMEM],
        out_specs=VMEM,
        compiler_params=pltpu.CompilerParams(vmem_limit_bytes=ROOM),
    )(block)


def hops(groups, count):
    return [(j, m) for j in range(count) for m in range(1, 2 if groups == 4 else groups)]


def body(probe, phase, row_offsets, col_offsets):
    size = probe.shape[-1]
    strip = phase.shape[1]
    count = row_offsets.shape[0]
    groups = lax.axis_size("depth")
    starts = jnp.stack([row_offsets - lax.axis_index("probe") * strip, col_offsets], axis=1)
    tables = operator_tables(size)
    own = coded(phase)
    following = {}
    for parity in (1, 0):
        following[parity] = handed_down(own, parity)
    arrived = {}
    after = []
    for parity in (0, 1):
        firsts = first_group(parity, starts, own, following[parity], probe, tables, after)
        blocks = [{0: first} for first in firsts]
        for j, m in hops(groups, count):
            blocks[j][m] = sent_on(firsts[j], (parity,), [(i, i ^ m) for i in range(groups) if i < i ^ m < groups])
        if parity == 0:
            after = [mark(firsts[-1])]
        arrived[parity] = blocks
    starting = [[] for _ in range(count)]
    if groups == 4:
        for j in range(count):
            starting[j].append(second_group(tables, arrived[0][j], arrived[1][j]))
        for target in (2, 3):
            for j in range(count):
                starting[j].append(sent_on(starting[j][0], (0, 1), [(1, target)]))
    finished = []
    for j in range(count):
        wave = chain(groups, tables, arrived[0][j], arrived[1][j], starting[j], finished if j == count - 1 else [])
        finished.append(wave)
    return wave[None]


def solution(mesh):
    return jax.shard_map(
        body,
        mesh=mesh,
        in_specs=(P(), P("depth", "probe", None), P("probe"), P("probe")),
        out_specs=P("depth", "probe", None, None, None),
        check_vma=False,
    )
```

```python
import functools
import math

import numpy as np
import jax
import jax.numpy as jnp
from jax import lax
from jax.experimental import pallas as pl
from jax.experimental.pallas import tpu as pltpu
from jax.sharding import PartitionSpec as P


CHIRP = 40.0
F32 = jnp.float32
BF16 = jnp.bfloat16
OCTAVES = 120.0
ROOM = 8 * 2**20


def handed_down(block, parity):
    strips = lax.axis_size("probe")
    return lax.ppermute(block, "probe", [(i + 1, i) for i in range(parity, strips - 1, 2)])


def sent_on(block, parities, pairs):
    strips = lax.axis_size("probe")
    route = [(a * strips + p, b * strips + p) for a, b in pairs for p in range(strips) if p % 2 in parities]
    return lax.ppermute(block, ("depth", "probe"), route)


def operator_tables(size):
    k = np.arange(size)
    freq = np.where(k < size // 2, k, k - size) / size
    taps = np.fft.ifft(np.exp(-1j * CHIRP * freq * freq))
    half = size // 2
    lag = (np.arange(half)[:, None] - np.arange(half)[None, :]) % size
    right, left = [], []
    for sign in (1.0, -1.0):
        part = 0.5 * (taps[lag] + sign * taps[(lag + half) % size])
        full = np.block([[part.real, part.imag], [-part.imag, part.real]]).astype(np.float32)
        high = full.astype(BF16)
        low = (full - high.astype(np.float32)).astype(BF16)
        right.append(np.concatenate([high, low], axis=0))
        left.append(np.concatenate([high.T, low.T], axis=1))
    return [jnp.asarray(np.stack(right)), jnp.asarray(np.stack(left))]


def fit(function, powers, reach):
    x = np.cos(np.pi * (np.arange(400) + 0.5) / 400) * reach
    basis = np.stack([(x / reach) ** p for p in powers], axis=1)
    found = np.linalg.lstsq(basis, function(x), rcond=None)[0]
    return [float(c / reach**p) for c, p in zip(found, powers)]


REACH = 0.5 * OCTAVES * math.log(2.0)


def half_angle(position):
    return position * (0.5 * math.pi / REACH)


SIN_FIT = fit(lambda y: math.sqrt(2.0) * np.sin(half_angle(y)), (1, 3, 5, 7), REACH)
COS_FIT = fit(lambda y: math.sqrt(2.0) * np.cos(half_angle(y)), (0, 2, 4, 6), REACH)


def horner(square, coefficients):
    value = coefficients[-1]
    for c in coefficients[-2::-1]:
        value = value * square + c
    return value


def phase_factor(code):
    position = jnp.log(code)
    square = position * position
    sine = position * horner(square, SIN_FIT)
    cosine = horner(square, COS_FIT)
    return 1.0 - sine * sine, sine * cosine


def coded(phase):
    turns = phase * (0.5 / math.pi)
    return jnp.exp2(OCTAVES * (turns - jnp.round(turns))).astype(BF16)


SMEM = pl.BlockSpec(memory_space=pltpu.SMEM)
VMEM = pl.BlockSpec(memory_space=pltpu.VMEM)


def product(a, b):
    return jnp.dot(a, b, preferred_element_type=F32)


def propagated(real, imag, right_ref, left_ref):
    size = real.shape[-1]
    half = size // 2

    def right(k, combine):
        data = jnp.concatenate([combine(real[:, :half], real[:, half:]), combine(imag[:, :half], imag[:, half:])], axis=1).astype(BF16)
        return product(data, right_ref[k, :size]) + product(data, right_ref[k, size:])

    plus, minus = right(0, jnp.add), right(1, jnp.subtract)
    re = jnp.concatenate([plus[:, :half], minus[:, :half]], axis=1)
    im = jnp.concatenate([plus[:, half:], minus[:, half:]], axis=1)

    def left(k, combine):
        data = jnp.concatenate([combine(re[:half], re[half:]), combine(im[:half], im[half:])], axis=0).astype(BF16)
        return product(left_ref[k, :, :size], data) + product(left_ref[k, :, size:], data)

    top, low = left(0, jnp.add), left(1, jnp.subtract)
    re = jnp.concatenate([top[:half] + low[:half], top[:half] - low[:half]], axis=0)
    im = jnp.concatenate([top[half:] + low[half:], top[half:] - low[half:]], axis=0)
    real = jnp.concatenate([re[:, :half] + re[:, half:], re[:, :half] - re[:, half:]], axis=1)
    imag = jnp.concatenate([im[:, :half] + im[:, half:], im[:, :half] - im[:, half:]], axis=1)
    return real, imag


def transmitted(real, imag, cosine, sine, right_ref, left_ref):
    real, imag = cosine * real - sine * imag, cosine * imag + sine * real
    return propagated(real, imag, right_ref, left_ref)


def sliced(real, imag, code, right_ref, left_ref):
    return transmitted(real, imag, *phase_factor(code.astype(F32)), right_ref, left_ref)


def window_kernel(count, parity, starts_ref, own_ref, next_ref, *refs):
    outs, scratch = refs[-1 - count : -1], refs[-1]
    layers, strip, width = own_ref.shape
    size = outs[0].shape[-1]
    span = size + 128
    place = lax.axis_index("probe")

    @pl.when(place % 2 == parity)
    def _():
        edge = (place == lax.axis_size("probe") - 1).astype(F32)
        line = lax.broadcasted_iota(jnp.int32, (strip, span), 0)
        for j, out in enumerate(outs):
            r = starts_ref[j, 0]
            c = starts_ref[j, 1]
            base = jnp.minimum(c // 128, (width - span) // 128)
            shift = c - base * 128
            lanes = pl.ds(pl.multiple_of(base * 128, 128), span)
            for s in range(layers):
                own = own_ref[s, :, lanes].astype(F32)
                following = next_ref[s, :, lanes].astype(F32) + edge
                merged = jnp.where(line >= r, own, following)
                turned = pltpu.roll(merged, span - shift, 1)[:, :size]
                for part in range(size // 128):
                    columns = turned[:, part * 128 : (part + 1) * 128]
                    scratch[part, pl.ds(0, strip), :] = columns
                    scratch[part, pl.ds(strip, strip), :] = columns
                    out[s, :, part * 128 : (part + 1) * 128] = scratch[part, pl.ds(r, size), :].astype(BF16)


def windows(parity, size, starts, own, following, after):
    layers, strip, _ = own.shape
    count = starts.shape[0]
    return pl.pallas_call(
        functools.partial(window_kernel, count, parity),
        out_shape=[jax.ShapeDtypeStruct((layers, size, size), BF16)] * count,
        in_specs=[SMEM] + [VMEM] * (2 + len(after)),
        out_specs=[VMEM] * count,
        scratch_shapes=[pltpu.VMEM((size // 128, 2 * strip, 128), F32)],
        compiler_params=pltpu.CompilerParams(vmem_limit_bytes=ROOM),
    )(starts, own, following, *after)


def rounded(state_ref, real, imag):
    state_ref[0] = real.astype(BF16).astype(F32)
    state_ref[1] = imag.astype(BF16).astype(F32)


def chain_kernel(groups, before, probe_ref, right_ref, left_ref, *refs):
    arrived = (refs[:groups], refs[groups : 2 * groups])
    out_ref, state_ref = refs[-2], refs[-1]
    group = lax.axis_index("depth")
    even = lax.axis_index("probe") % 2 == 0

    def block(g, s):
        value = None
        for m in sorted({g ^ own for own in range(g, groups)}):
            this = jnp.where(even, arrived[0][m][s], arrived[1][m][s])
            value = this if value is None else jnp.where(group ^ g == m, this, value)
        return value

    state_ref[...] = probe_ref[...]
    for g in range(groups):

        @pl.when(g <= group)
        def _():
            real, imag = state_ref[0], state_ref[1]
            for s in range(arrived[0][0].shape[0]):
                real, imag = sliced(real, imag, block(g, s), right_ref, left_ref)
            rounded(state_ref, real, imag)

    out_ref[before] = state_ref[...].astype(BF16)
    for j in range(before):
        out_ref[j] = refs[2 * groups + j][0]


def chain(groups, probe, tables, even, odd, finished):
    blocks = [each[m] for each in (even, odd) for m in range(groups)]
    arguments = [probe, *tables, *blocks, *finished]
    return pl.pallas_call(
        functools.partial(chain_kernel, groups, len(finished)),
        out_shape=jax.ShapeDtypeStruct((len(finished) + 1, *probe.shape), BF16),
        in_specs=[VMEM] * len(arguments),
        out_specs=VMEM,
        scratch_shapes=[pltpu.VMEM(probe.shape, F32)],
        compiler_params=pltpu.CompilerParams(vmem_limit_bytes=ROOM),
    )(*arguments)


def factor_kernel(count, unused, *refs):
    even_refs, odd_refs, outs = refs[:count], refs[count : 2 * count], refs[2 * count :]
    even = lax.axis_index("probe") % 2 == 0
    group = lax.axis_index("depth")

    @pl.when(group != unused)
    def _():
        for j in range(count):
            for s in range(even_refs[j].shape[0]):
                code = jnp.where(even, even_refs[j][s], odd_refs[j][s])
                outs[j][s, 0], outs[j][s, 1] = phase_factor(code.astype(F32))


def phase_factors(unused, even, odd):
    count = len(even)
    layers, size, _ = even[0].shape
    return pl.pallas_call(
        functools.partial(factor_kernel, count, unused),
        out_shape=[jax.ShapeDtypeStruct((layers, 2, size, size), F32)] * count,
        in_specs=[VMEM] * (2 * count),
        out_specs=[VMEM] * count,
        compiler_params=pltpu.CompilerParams(vmem_limit_bytes=ROOM),
    )(*even, *odd)


def group_of(state_ref, factor, layers, right_ref, left_ref):
    real, imag = state_ref[0], state_ref[1]
    for s in range(layers):
        real, imag = transmitted(real, imag, factor(s, 0), factor(s, 1), right_ref, left_ref)
    rounded(state_ref, real, imag)


def second_kernel(probe_ref, right_ref, left_ref, own_ref, near_ref, first_ref, second_ref, state_ref):
    group = lax.axis_index("depth")

    @pl.when(group < 2)
    def _():
        state_ref[...] = probe_ref[...]
        for g, out_ref in enumerate((first_ref, second_ref)):
            factor = lambda s, k: jnp.where(group == g, own_ref[s, k], near_ref[s, k])
            group_of(state_ref, factor, own_ref.shape[0], right_ref, left_ref)
            out_ref[...] = state_ref[...].astype(BF16)


def second_group(probe, tables, own, near):
    return pl.pallas_call(
        second_kernel,
        out_shape=[jax.ShapeDtypeStruct(probe.shape, BF16)] * 2,
        in_specs=[VMEM] * 5,
        out_specs=[VMEM] * 2,
        scratch_shapes=[pltpu.VMEM(probe.shape, F32)],
        compiler_params=pltpu.CompilerParams(vmem_limit_bytes=ROOM),
    )(probe, *tables, own, near)


def last_kernel(right_ref, left_ref, own_ref, near_ref, first_ref, second_ref, far_ref, *refs):
    out_ref, state_ref = refs[-2:]
    finished = refs[:-2]
    layers = own_ref.shape[0]
    group = lax.axis_index("depth")
    for part in range(2):
        value = jnp.where(group == 0, first_ref[part], second_ref[part])
        value = jnp.where(group >= 2, far_ref[part], value)
        state_ref[part] = value.astype(F32)

    @pl.when(group == 3)
    def _():
        group_of(state_ref, lambda s, k: near_ref[s, k], layers, right_ref, left_ref)

    @pl.when(group >= 2)
    def _():
        group_of(state_ref, lambda s, k: own_ref[s, k], layers, right_ref, left_ref)

    out_ref[len(finished)] = state_ref[...].astype(BF16)
    for j, ref in enumerate(finished):
        out_ref[j] = ref[0]


def last_groups(tables, own, near, waves, finished):
    shape = waves[0].shape
    arguments = [*tables, own, near, *waves, *finished]
    return pl.pallas_call(
        last_kernel,
        out_shape=jax.ShapeDtypeStruct((len(finished) + 1, *shape), BF16),
        in_specs=[VMEM] * len(arguments),
        out_specs=VMEM,
        scratch_shapes=[pltpu.VMEM(shape, F32)],
        compiler_params=pltpu.CompilerParams(vmem_limit_bytes=ROOM),
    )(*arguments)


def mark_kernel(block_ref, out_ref):
    out_ref[...] = block_ref[0, :16, :128]


def mark(block):
    return pl.pallas_call(
        mark_kernel,
        out_shape=jax.ShapeDtypeStruct((16, 128), BF16),
        in_specs=[VMEM],
        out_specs=VMEM,
        compiler_params=pltpu.CompilerParams(vmem_limit_bytes=ROOM),
    )(block)


def pairs_at(groups, m):
    if groups == 4:
        return [(0, 1), (1, 0), (2, 3)]
    return [(i, i ^ m) for i in range(groups) if i < i ^ m < groups]


def hops(groups, count):
    return [(j, m) for j in range(count) for m in range(1, 2 if groups == 4 else groups)]


def body(probe, phase, row_offsets, col_offsets):
    size = probe.shape[-1]
    strip = phase.shape[1]
    count = row_offsets.shape[0]
    groups = lax.axis_size("depth")
    starts = jnp.stack([row_offsets - lax.axis_index("probe") * strip, col_offsets], axis=1)
    tables = operator_tables(size)
    own = coded(phase)
    following = {}
    for parity in (1, 0):
        following[parity] = handed_down(own, parity)
    arrived = {}
    after = []
    for parity in (0, 1):
        firsts = windows(parity, size, starts, own, following[parity], after)
        blocks = [{0: first} for first in firsts]
        for j, m in hops(groups, count):
            blocks[j][m] = sent_on(firsts[j], (parity,), pairs_at(groups, m))
        if parity == 0:
            after = [mark(firsts[-1])]
        arrived[parity] = blocks
    if groups == 4:
        return four_groups(probe, tables, arrived)[None]
    finished = []
    for j in range(count):
        wave = chain(groups, probe, tables, arrived[0][j], arrived[1][j], finished if j == count - 1 else [])
        finished.append(wave)
    return wave[None]


def four_groups(probe, tables, arrived):
    even, odd = arrived[0], arrived[1]
    count = len(even)
    own = phase_factors(-1, [b[0] for b in even], [b[0] for b in odd])
    near, waves = [], []
    for j in range(count):
        near += phase_factors(2, [even[j][1]], [odd[j][1]])
        waves.append([*second_group(probe, tables, own[j], near[j])])
        waves[j].append(sent_on(waves[j][1], (0, 1), [(0, 2), (1, 3)]))
    finished = []
    for j in range(count):
        wave = last_groups(tables, own[j], near[j], waves[j], finished if j == count - 1 else [])
        finished.append(wave)
    return wave


def solution(mesh):
    return jax.shard_map(
        body,
        mesh=mesh,
        in_specs=(P(), P("depth", "probe", None), P("probe"), P("probe")),
        out_specs=P("depth", "probe", None, None, None),
        check_vma=False,
    )
```

```python
import functools
import math

import numpy as np
import jax
import jax.numpy as jnp
from jax import lax
from jax.experimental import pallas as pl
from jax.experimental.pallas import tpu as pltpu
from jax.sharding import PartitionSpec as P


CHIRP = 40.0
F32 = jnp.float32
BF16 = jnp.bfloat16
OCTAVES = 120.0
ROOM = 8 * 2**20


def handed_down(block, parity):
    strips = lax.axis_size("probe")
    return lax.ppermute(block, "probe", [(i + 1, i) for i in range(parity, strips - 1, 2)])


def sent_on(block, parities, pairs):
    strips = lax.axis_size("probe")
    route = [(a * strips + p, b * strips + p) for a, b in pairs for p in range(strips) if p % 2 in parities]
    return lax.ppermute(block, ("depth", "probe"), route)


def operator_tables(size):
    k = np.arange(size)
    freq = np.where(k < size // 2, k, k - size) / size
    taps = np.fft.ifft(np.exp(-1j * CHIRP * freq * freq))
    half = size // 2
    lag = (np.arange(half)[:, None] - np.arange(half)[None, :]) % size
    right, left = [], []
    for sign in (1.0, -1.0):
        part = 0.5 * (taps[lag] + sign * taps[(lag + half) % size])
        full = np.block([[part.real, part.imag], [-part.imag, part.real]]).astype(np.float32)
        high = full.astype(BF16)
        low = (full - high.astype(np.float32)).astype(BF16)
        right.append(np.concatenate([high, low], axis=0))
        left.append(np.concatenate([high.T, low.T], axis=1))
    return [jnp.asarray(np.stack(right)), jnp.asarray(np.stack(left))]


def fit(function, powers, reach):
    x = np.cos(np.pi * (np.arange(400) + 0.5) / 400) * reach
    basis = np.stack([(x / reach) ** p for p in powers], axis=1)
    found = np.linalg.lstsq(basis, function(x), rcond=None)[0]
    return [float(c / reach**p) for c, p in zip(found, powers)]


REACH = 0.5 * OCTAVES * math.log(2.0)


def half_angle(position):
    return position * (0.5 * math.pi / REACH)


SIN_FIT = fit(lambda y: math.sqrt(2.0) * np.sin(half_angle(y)), (1, 3, 5, 7), REACH)
COS_FIT = fit(lambda y: math.sqrt(2.0) * np.cos(half_angle(y)), (0, 2, 4, 6), REACH)


def horner(square, coefficients):
    value = coefficients[-1]
    for c in coefficients[-2::-1]:
        value = value * square + c
    return value


def phase_factor(code):
    position = jnp.log(code)
    square = position * position
    sine = position * horner(square, SIN_FIT)
    cosine = horner(square, COS_FIT)
    return 1.0 - sine * sine, sine * cosine


def coded(phase):
    turns = phase * (0.5 / math.pi)
    return jnp.exp2(OCTAVES * (turns - jnp.round(turns))).astype(BF16)


SMEM = pl.BlockSpec(memory_space=pltpu.SMEM)
VMEM = pl.BlockSpec(memory_space=pltpu.VMEM)


def product(a, b):
    return jnp.dot(a, b, preferred_element_type=F32)


def propagated(real, imag, right_ref, left_ref):
    size = real.shape[-1]
    half = size // 2

    def right(k, combine):
        data = jnp.concatenate([combine(real[:, :half], real[:, half:]), combine(imag[:, :half], imag[:, half:])], axis=1).astype(BF16)
        return product(data, right_ref[k, :size]) + product(data, right_ref[k, size:])

    plus, minus = right(0, jnp.add), right(1, jnp.subtract)
    re = jnp.concatenate([plus[:, :half], minus[:, :half]], axis=1)
    im = jnp.concatenate([plus[:, half:], minus[:, half:]], axis=1)

    def left(k, combine):
        data = jnp.concatenate([combine(re[:half], re[half:]), combine(im[:half], im[half:])], axis=0).astype(BF16)
        return product(left_ref[k, :, :size], data) + product(left_ref[k, :, size:], data)

    top, low = left(0, jnp.add), left(1, jnp.subtract)
    re = jnp.concatenate([top[:half] + low[:half], top[:half] - low[:half]], axis=0)
    im = jnp.concatenate([top[half:] + low[half:], top[half:] - low[half:]], axis=0)
    real = jnp.concatenate([re[:, :half] + re[:, half:], re[:, :half] - re[:, half:]], axis=1)
    imag = jnp.concatenate([im[:, :half] + im[:, half:], im[:, :half] - im[:, half:]], axis=1)
    return real, imag


def transmitted(real, imag, cosine, sine, right_ref, left_ref):
    real, imag = cosine * real - sine * imag, cosine * imag + sine * real
    return propagated(real, imag, right_ref, left_ref)


def sliced(real, imag, code, right_ref, left_ref):
    return transmitted(real, imag, *phase_factor(code.astype(F32)), right_ref, left_ref)


def window_kernel(count, parity, starts_ref, own_ref, next_ref, *refs):
    outs, scratch = refs[-1 - count : -1], refs[-1]
    layers, strip, width = own_ref.shape
    size = outs[0].shape[-1]
    span = size + 128
    place = lax.axis_index("probe")

    @pl.when(place % 2 == parity)
    def _():
        edge = (place == lax.axis_size("probe") - 1).astype(F32)
        line = lax.broadcasted_iota(jnp.int32, (strip, span), 0)
        for j, out in enumerate(outs):
            r = jnp.max(starts_ref[j, 0]).astype(jnp.int32)
            c = jnp.max(starts_ref[j, 1]).astype(jnp.int32)
            base = jnp.minimum(c // 128, (width - span) // 128)
            shift = c - base * 128
            lanes = pl.ds(pl.multiple_of(base * 128, 128), span)
            for s in range(layers):
                own = own_ref[s, :, lanes].astype(F32)
                following = next_ref[s, :, lanes].astype(F32) + edge
                merged = jnp.where(line >= r, own, following)
                turned = pltpu.roll(merged, span - shift, 1)[:, :size]
                for part in range(size // 128):
                    columns = turned[:, part * 128 : (part + 1) * 128]
                    scratch[part, pl.ds(0, strip), :] = columns
                    scratch[part, pl.ds(strip, strip), :] = columns
                    out[s, :, part * 128 : (part + 1) * 128] = scratch[part, pl.ds(r, size), :].astype(BF16)


def windows(parity, size, starts, own, following, after):
    layers, strip, _ = own.shape
    count = starts.shape[0]
    return pl.pallas_call(
        functools.partial(window_kernel, count, parity),
        out_shape=[jax.ShapeDtypeStruct((layers, size, size), BF16)] * count,
        in_specs=[VMEM] * (3 + len(after)),
        out_specs=[VMEM] * count,
        scratch_shapes=[pltpu.VMEM((size // 128, 2 * strip, 128), F32)],
        compiler_params=pltpu.CompilerParams(vmem_limit_bytes=ROOM),
    )(starts, own, following, *after)


def rounded(state_ref, real, imag):
    state_ref[0] = real.astype(BF16).astype(F32)
    state_ref[1] = imag.astype(BF16).astype(F32)


def chain_kernel(groups, before, probe_ref, right_ref, left_ref, *refs):
    arrived = (refs[:groups], refs[groups : 2 * groups])
    out_ref, state_ref = refs[-2], refs[-1]
    group = lax.axis_index("depth")
    even = lax.axis_index("probe") % 2 == 0

    def block(g, s):
        value = None
        for m in sorted({g ^ own for own in range(g, groups)}):
            this = jnp.where(even, arrived[0][m][s], arrived[1][m][s])
            value = this if value is None else jnp.where(group ^ g == m, this, value)
        return value

    state_ref[...] = probe_ref[...]
    for g in range(groups):

        @pl.when(g <= group)
        def _():
            real, imag = state_ref[0], state_ref[1]
            for s in range(arrived[0][0].shape[0]):
                real, imag = sliced(real, imag, block(g, s), right_ref, left_ref)
            rounded(state_ref, real, imag)

    out_ref[before] = state_ref[...].astype(BF16)
    for j in range(before):
        out_ref[j] = refs[2 * groups + j][0]


def chain(groups, probe, tables, even, odd, finished):
    blocks = [each[m] for each in (even, odd) for m in range(groups)]
    arguments = [probe, *tables, *blocks, *finished]
    return pl.pallas_call(
        functools.partial(chain_kernel, groups, len(finished)),
        out_shape=jax.ShapeDtypeStruct((len(finished) + 1, *probe.shape), BF16),
        in_specs=[VMEM] * len(arguments),
        out_specs=VMEM,
        scratch_shapes=[pltpu.VMEM(probe.shape, F32)],
        compiler_params=pltpu.CompilerParams(vmem_limit_bytes=ROOM),
    )(*arguments)


def factor_kernel(count, unused, *refs):
    even_refs, odd_refs, outs = refs[:count], refs[count : 2 * count], refs[2 * count :]
    even = lax.axis_index("probe") % 2 == 0
    group = lax.axis_index("depth")

    @pl.when(group != unused)
    def _():
        for j in range(count):
            for s in range(even_refs[j].shape[0]):
                code = jnp.where(even, even_refs[j][s], odd_refs[j][s])
                outs[j][s, 0], outs[j][s, 1] = phase_factor(code.astype(F32))


def phase_factors(unused, even, odd):
    count = len(even)
    layers, size, _ = even[0].shape
    return pl.pallas_call(
        functools.partial(factor_kernel, count, unused),
        out_shape=[jax.ShapeDtypeStruct((layers, 2, size, size), F32)] * count,
        in_specs=[VMEM] * (2 * count),
        out_specs=[VMEM] * count,
        compiler_params=pltpu.CompilerParams(vmem_limit_bytes=ROOM),
    )(*even, *odd)


def group_of(state_ref, factor, layers, right_ref, left_ref):
    real, imag = state_ref[0], state_ref[1]
    for s in range(layers):
        real, imag = transmitted(real, imag, factor(s, 0), factor(s, 1), right_ref, left_ref)
    rounded(state_ref, real, imag)


def second_kernel(probe_ref, right_ref, left_ref, own_ref, near_ref, first_ref, second_ref, state_ref):
    group = lax.axis_index("depth")

    @pl.when(group < 2)
    def _():
        state_ref[...] = probe_ref[...]
        for g, out_ref in enumerate((first_ref, second_ref)):
            factor = lambda s, k: jnp.where(group == g, own_ref[s, k], near_ref[s, k])
            group_of(state_ref, factor, own_ref.shape[0], right_ref, left_ref)
            out_ref[...] = state_ref[...].astype(BF16)


def second_group(probe, tables, own, near):
    return pl.pallas_call(
        second_kernel,
        out_shape=[jax.ShapeDtypeStruct(probe.shape, BF16)] * 2,
        in_specs=[VMEM] * 5,
        out_specs=[VMEM] * 2,
        scratch_shapes=[pltpu.VMEM(probe.shape, F32)],
        compiler_params=pltpu.CompilerParams(vmem_limit_bytes=ROOM),
    )(probe, *tables, own, near)


def last_kernel(right_ref, left_ref, own_ref, near_ref, first_ref, second_ref, far_ref, *refs):
    out_ref, state_ref = refs[-2:]
    finished = refs[:-2]
    layers = own_ref.shape[0]
    group = lax.axis_index("depth")
    for part in range(2):
        value = jnp.where(group == 0, first_ref[part], second_ref[part])
        value = jnp.where(group >= 2, far_ref[part], value)
        state_ref[part] = value.astype(F32)

    @pl.when(group == 3)
    def _():
        group_of(state_ref, lambda s, k: near_ref[s, k], layers, right_ref, left_ref)

    @pl.when(group >= 2)
    def _():
        group_of(state_ref, lambda s, k: own_ref[s, k], layers, right_ref, left_ref)

    out_ref[len(finished)] = state_ref[...].astype(BF16)
    for j, ref in enumerate(finished):
        out_ref[j] = ref[0]


def last_groups(tables, own, near, waves, finished):
    shape = waves[0].shape
    arguments = [*tables, own, near, *waves, *finished]
    return pl.pallas_call(
        last_kernel,
        out_shape=jax.ShapeDtypeStruct((len(finished) + 1, *shape), BF16),
        in_specs=[VMEM] * len(arguments),
        out_specs=VMEM,
        scratch_shapes=[pltpu.VMEM(shape, F32)],
        compiler_params=pltpu.CompilerParams(vmem_limit_bytes=ROOM),
    )(*arguments)


def mark_kernel(block_ref, out_ref):
    out_ref[...] = block_ref[0, :16, :128]


def mark(block):
    return pl.pallas_call(
        mark_kernel,
        out_shape=jax.ShapeDtypeStruct((16, 128), BF16),
        in_specs=[VMEM],
        out_specs=VMEM,
        compiler_params=pltpu.CompilerParams(vmem_limit_bytes=ROOM),
    )(block)


def pairs_at(groups, m):
    if groups == 4:
        return [(0, 1), (1, 0), (2, 3)]
    return [(i, i ^ m) for i in range(groups) if i < i ^ m < groups]


def hops(groups, count):
    return [(j, m) for j in range(count) for m in range(1, 2 if groups == 4 else groups)]


def body(probe, phase, row_offsets, col_offsets):
    size = probe.shape[-1]
    strip = phase.shape[1]
    count = row_offsets.shape[0]
    groups = lax.axis_size("depth")
    starts = jnp.stack([row_offsets - lax.axis_index("probe") * strip, col_offsets], axis=1)
    starts = jnp.broadcast_to(starts.astype(F32)[:, :, None, None], (count, 2, 8, 128))
    tables = operator_tables(size)
    own = coded(phase)
    following = {}
    for parity in (1, 0):
        following[parity] = handed_down(own, parity)
    arrived = {}
    after = []
    for parity in (0, 1):
        firsts = windows(parity, size, starts, own, following[parity], after)
        blocks = [{0: first} for first in firsts]
        for j, m in hops(groups, count):
            blocks[j][m] = sent_on(firsts[j], (parity,), pairs_at(groups, m))
        if parity == 0:
            after = [mark(firsts[-1])]
        arrived[parity] = blocks
    if groups == 4:
        return four_groups(probe, tables, arrived)[None]
    finished = []
    for j in range(count):
        wave = chain(groups, probe, tables, arrived[0][j], arrived[1][j], finished if j == count - 1 else [])
        finished.append(wave)
    return wave[None]


def four_groups(probe, tables, arrived):
    even, odd = arrived[0], arrived[1]
    count = len(even)
    own = phase_factors(-1, [b[0] for b in even], [b[0] for b in odd])
    near, waves = [], []
    for j in range(count):
        near += phase_factors(2, [even[j][1]], [odd[j][1]])
        waves.append([*second_group(probe, tables, own[j], near[j])])
        waves[j].append(sent_on(waves[j][1], (0, 1), [(0, 2), (1, 3)]))
    finished = []
    for j in range(count):
        wave = last_groups(tables, own[j], near[j], waves[j], finished if j == count - 1 else [])
        finished.append(wave)
    return wave


def solution(mesh):
    return jax.shard_map(
        body,
        mesh=mesh,
        in_specs=(P(), P("depth", "probe", None), P("probe"), P("probe")),
        out_specs=P("depth", "probe", None, None, None),
        check_vma=False,
    )
```

```python
import functools
import math

import numpy as np
import jax
import jax.numpy as jnp
from jax import lax
from jax.experimental import pallas as pl
from jax.experimental.pallas import tpu as pltpu
from jax.sharding import PartitionSpec as P


CHIRP = 40.0
F32 = jnp.float32
BF16 = jnp.bfloat16
OCTAVES = 120.0
ROOM = 8 * 2**20


def handed_down(block, parity):
    strips = lax.axis_size("probe")
    return lax.ppermute(block, "probe", [(i + 1, i) for i in range(parity, strips - 1, 2)])


def sent_on(block, parities, pairs):
    strips = lax.axis_size("probe")
    route = [(a * strips + p, b * strips + p) for a, b in pairs for p in range(strips) if p % 2 in parities]
    return lax.ppermute(block, ("depth", "probe"), route)


def operator_tables(size):
    k = np.arange(size)
    freq = np.where(k < size // 2, k, k - size) / size
    taps = np.fft.ifft(np.exp(-1j * CHIRP * freq * freq))
    half = size // 2
    lag = (np.arange(half)[:, None] - np.arange(half)[None, :]) % size
    right, left = [], []
    for sign in (1.0, -1.0):
        part = 0.5 * (taps[lag] + sign * taps[(lag + half) % size])
        full = np.block([[part.real, part.imag], [-part.imag, part.real]]).astype(np.float32)
        high = full.astype(BF16)
        low = (full - high.astype(np.float32)).astype(BF16)
        right.append(np.concatenate([high, low], axis=0))
        left.append(np.concatenate([high.T, low.T], axis=1))
    return [jnp.asarray(np.stack(right)), jnp.asarray(np.stack(left))]


def fit(function, powers, reach):
    x = np.cos(np.pi * (np.arange(400) + 0.5) / 400) * reach
    basis = np.stack([(x / reach) ** p for p in powers], axis=1)
    found = np.linalg.lstsq(basis, function(x), rcond=None)[0]
    return [float(c / reach**p) for c, p in zip(found, powers)]


REACH = 0.5 * OCTAVES * math.log(2.0)


def half_angle(position):
    return position * (0.5 * math.pi / REACH)


SIN_FIT = fit(lambda y: math.sqrt(2.0) * np.sin(half_angle(y)), (1, 3, 5, 7), REACH)
COS_FIT = fit(lambda y: math.sqrt(2.0) * np.cos(half_angle(y)), (0, 2, 4, 6), REACH)


def horner(square, coefficients):
    value = coefficients[-1]
    for c in coefficients[-2::-1]:
        value = value * square + c
    return value


def phase_factor(code):
    position = jnp.log(code)
    square = position * position
    sine = position * horner(square, SIN_FIT)
    cosine = horner(square, COS_FIT)
    return 1.0 - sine * sine, sine * cosine


def coded(phase):
    turns = phase * (0.5 / math.pi)
    return jnp.exp2(OCTAVES * (turns - jnp.round(turns))).astype(BF16)


SMEM = pl.BlockSpec(memory_space=pltpu.SMEM)
VMEM = pl.BlockSpec(memory_space=pltpu.VMEM)


def product(a, b):
    return jnp.dot(a, b, preferred_element_type=F32)


def propagated(real, imag, right_ref, left_ref):
    size = real.shape[-1]
    half = size // 2

    def right(k, combine):
        data = jnp.concatenate([combine(real[:, :half], real[:, half:]), combine(imag[:, :half], imag[:, half:])], axis=1).astype(BF16)
        return product(data, right_ref[k, :size]) + product(data, right_ref[k, size:])

    plus, minus = right(0, jnp.add), right(1, jnp.subtract)
    re = jnp.concatenate([plus[:, :half], minus[:, :half]], axis=1)
    im = jnp.concatenate([plus[:, half:], minus[:, half:]], axis=1)

    def left(k, combine):
        data = jnp.concatenate([combine(re[:half], re[half:]), combine(im[:half], im[half:])], axis=0).astype(BF16)
        return product(left_ref[k, :, :size], data) + product(left_ref[k, :, size:], data)

    top, low = left(0, jnp.add), left(1, jnp.subtract)
    re = jnp.concatenate([top[:half] + low[:half], top[:half] - low[:half]], axis=0)
    im = jnp.concatenate([top[half:] + low[half:], top[half:] - low[half:]], axis=0)
    real = jnp.concatenate([re[:, :half] + re[:, half:], re[:, :half] - re[:, half:]], axis=1)
    imag = jnp.concatenate([im[:, :half] + im[:, half:], im[:, :half] - im[:, half:]], axis=1)
    return real, imag


def transmitted(real, imag, cosine, sine, right_ref, left_ref):
    real, imag = cosine * real - sine * imag, cosine * imag + sine * real
    return propagated(real, imag, right_ref, left_ref)


def sliced(real, imag, code, right_ref, left_ref):
    return transmitted(real, imag, *phase_factor(code.astype(F32)), right_ref, left_ref)


def window_kernel(count, parity, starts_ref, own_ref, next_ref, *refs):
    outs, scratch = refs[-1 - count : -1], refs[-1]
    layers, strip, width = own_ref.shape
    size = outs[0].shape[-1]
    span = size + 128
    place = lax.axis_index("probe")

    @pl.when(place % 2 == parity)
    def _():
        edge = (place == lax.axis_size("probe") - 1).astype(F32)
        line = lax.broadcasted_iota(jnp.int32, (strip, span), 0)
        for j, out in enumerate(outs):
            r = starts_ref[j, 0]
            c = starts_ref[j, 1]
            base = jnp.minimum(c // 128, (width - span) // 128)
            shift = c - base * 128
            lanes = pl.ds(pl.multiple_of(base * 128, 128), span)
            for s in range(layers):
                own = own_ref[s, :, lanes].astype(F32)
                following = next_ref[s, :, lanes].astype(F32) + edge
                merged = jnp.where(line >= r, own, following)
                turned = pltpu.roll(merged, span - shift, 1)[:, :size]
                for part in range(size // 128):
                    columns = turned[:, part * 128 : (part + 1) * 128]
                    scratch[part, pl.ds(0, strip), :] = columns
                    scratch[part, pl.ds(strip, strip), :] = columns
                    out[s, :, part * 128 : (part + 1) * 128] = scratch[part, pl.ds(r, size), :].astype(BF16)


def windows(parity, size, starts, own, following, after):
    layers, strip, _ = own.shape
    count = starts.shape[0]
    return pl.pallas_call(
        functools.partial(window_kernel, count, parity),
        out_shape=[jax.ShapeDtypeStruct((layers, size, size), BF16)] * count,
        in_specs=[SMEM] + [VMEM] * (2 + len(after)),
        out_specs=[VMEM] * count,
        scratch_shapes=[pltpu.VMEM((size // 128, 2 * strip, 128), F32)],
        compiler_params=pltpu.CompilerParams(vmem_limit_bytes=ROOM),
    )(starts, own, following, *after)


def rounded(state_ref, real, imag):
    state_ref[0] = real.astype(BF16).astype(F32)
    state_ref[1] = imag.astype(BF16).astype(F32)


def chain_kernel(groups, before, probe_ref, right_ref, left_ref, *refs):
    arrived = (refs[:groups], refs[groups : 2 * groups])
    out_ref, state_ref = refs[-2], refs[-1]
    group = lax.axis_index("depth")
    even = lax.axis_index("probe") % 2 == 0

    def block(g, s):
        value = None
        for m in sorted({g ^ own for own in range(g, groups)}):
            this = jnp.where(even, arrived[0][m][s], arrived[1][m][s])
            value = this if value is None else jnp.where(group ^ g == m, this, value)
        return value

    state_ref[...] = probe_ref[...]
    for g in range(groups):

        @pl.when(g <= group)
        def _():
            real, imag = state_ref[0], state_ref[1]
            for s in range(arrived[0][0].shape[0]):
                real, imag = sliced(real, imag, block(g, s), right_ref, left_ref)
            rounded(state_ref, real, imag)

    out_ref[before] = state_ref[...].astype(BF16)
    for j in range(before):
        out_ref[j] = refs[2 * groups + j][0]


def chain(groups, probe, tables, even, odd, finished):
    blocks = [each[m] for each in (even, odd) for m in range(groups)]
    arguments = [probe, *tables, *blocks, *finished]
    return pl.pallas_call(
        functools.partial(chain_kernel, groups, len(finished)),
        out_shape=jax.ShapeDtypeStruct((len(finished) + 1, *probe.shape), BF16),
        in_specs=[VMEM] * len(arguments),
        out_specs=VMEM,
        scratch_shapes=[pltpu.VMEM(probe.shape, F32)],
        compiler_params=pltpu.CompilerParams(vmem_limit_bytes=ROOM),
    )(*arguments)


def factor_kernel(count, unused, *refs):
    even_refs, odd_refs, outs = refs[:count], refs[count : 2 * count], refs[2 * count :]
    even = lax.axis_index("probe") % 2 == 0
    group = lax.axis_index("depth")

    @pl.when(group != unused)
    def _():
        for j in range(count):
            for s in range(even_refs[j].shape[0]):
                code = jnp.where(even, even_refs[j][s], odd_refs[j][s])
                outs[j][s, 0], outs[j][s, 1] = phase_factor(code.astype(F32))


def phase_factors(unused, even, odd):
    count = len(even)
    layers, size, _ = even[0].shape
    return pl.pallas_call(
        functools.partial(factor_kernel, count, unused),
        out_shape=[jax.ShapeDtypeStruct((layers, 2, size, size), F32)] * count,
        in_specs=[VMEM] * (2 * count),
        out_specs=[VMEM] * count,
        compiler_params=pltpu.CompilerParams(vmem_limit_bytes=ROOM),
    )(*even, *odd)


def group_of(state_ref, factor, layers, right_ref, left_ref):
    real, imag = state_ref[0], state_ref[1]
    for s in range(layers):
        real, imag = transmitted(real, imag, factor(s, 0), factor(s, 1), right_ref, left_ref)
    rounded(state_ref, real, imag)


def second_kernel(probe_ref, right_ref, left_ref, own_ref, near_ref, first_ref, second_ref, state_ref):
    group = lax.axis_index("depth")

    @pl.when(group < 2)
    def _():
        state_ref[...] = probe_ref[...]
        for g, out_ref in enumerate((first_ref, second_ref)):
            factor = lambda s, k: jnp.where(group == g, own_ref[s, k], near_ref[s, k])
            group_of(state_ref, factor, own_ref.shape[0], right_ref, left_ref)
            out_ref[...] = state_ref[...].astype(BF16)


def second_group(probe, tables, own, near):
    return pl.pallas_call(
        second_kernel,
        out_shape=[jax.ShapeDtypeStruct(probe.shape, BF16)] * 2,
        in_specs=[VMEM] * 5,
        out_specs=[VMEM] * 2,
        scratch_shapes=[pltpu.VMEM(probe.shape, F32)],
        compiler_params=pltpu.CompilerParams(vmem_limit_bytes=ROOM),
    )(probe, *tables, own, near)


def last_kernel(before, right_ref, left_ref, own_ref, near_ref, first_ref, second_ref, far_ref, *refs):
    finished = refs[:before]
    out_ref, state_ref = refs[before : before + 2]
    copies = []
    if before:
        wave_ref, done = refs[before + 2 :]
        copies = [pltpu.make_async_copy(ref.at[0], out_ref.at[j], done.at[j]) for j, ref in enumerate(finished)]
    for copy in copies:
        copy.start()
    layers = own_ref.shape[0]
    group = lax.axis_index("depth")
    for part in range(2):
        value = jnp.where(group == 0, first_ref[part], second_ref[part])
        value = jnp.where(group >= 2, far_ref[part], value)
        state_ref[part] = value.astype(F32)

    @pl.when(group == 3)
    def _():
        group_of(state_ref, lambda s, k: near_ref[s, k], layers, right_ref, left_ref)

    @pl.when(group >= 2)
    def _():
        group_of(state_ref, lambda s, k: own_ref[s, k], layers, right_ref, left_ref)

    if before:
        wave_ref[...] = state_ref[...].astype(BF16)
        copies.append(pltpu.make_async_copy(wave_ref, out_ref.at[before], done.at[before]))
        copies[-1].start()
    else:
        out_ref[0] = state_ref[...].astype(BF16)
    for copy in copies:
        copy.wait()


def last_groups(tables, own, near, waves, finished):
    shape = waves[0].shape
    before = len(finished)
    scratch = [pltpu.VMEM(shape, F32)]
    if before:
        scratch += [pltpu.VMEM(shape, BF16), pltpu.SemaphoreType.DMA((before + 1,))]
    arguments = [*tables, own, near, *waves, *finished]
    return pl.pallas_call(
        functools.partial(last_kernel, before),
        out_shape=jax.ShapeDtypeStruct((len(finished) + 1, *shape), BF16),
        in_specs=[VMEM] * len(arguments),
        out_specs=pl.BlockSpec(memory_space=pl.ANY) if before else VMEM,
        scratch_shapes=scratch,
        compiler_params=pltpu.CompilerParams(vmem_limit_bytes=ROOM),
    )(*arguments)


def mark_kernel(block_ref, out_ref):
    out_ref[...] = block_ref[0, :16, :128]


def mark(block):
    return pl.pallas_call(
        mark_kernel,
        out_shape=jax.ShapeDtypeStruct((16, 128), BF16),
        in_specs=[VMEM],
        out_specs=VMEM,
        compiler_params=pltpu.CompilerParams(vmem_limit_bytes=ROOM),
    )(block)


def pairs_at(groups, m):
    if groups == 4:
        return [(0, 1), (1, 0), (2, 3)]
    return [(i, i ^ m) for i in range(groups) if i < i ^ m < groups]


def hops(groups, count):
    return [(j, m) for j in range(count) for m in range(1, 2 if groups == 4 else groups)]


def body(probe, phase, row_offsets, col_offsets):
    size = probe.shape[-1]
    strip = phase.shape[1]
    count = row_offsets.shape[0]
    groups = lax.axis_size("depth")
    starts = jnp.stack([row_offsets - lax.axis_index("probe") * strip, col_offsets], axis=1)
    tables = operator_tables(size)
    own = coded(phase)
    following = {}
    for parity in (1, 0):
        following[parity] = handed_down(own, parity)
    arrived = {}
    after = []
    for parity in (0, 1):
        firsts = windows(parity, size, starts, own, following[parity], after)
        blocks = [{0: first} for first in firsts]
        for j, m in hops(groups, count):
            blocks[j][m] = sent_on(firsts[j], (parity,), pairs_at(groups, m))
        if parity == 0:
            after = [mark(firsts[-1])]
        arrived[parity] = blocks
    if groups == 4:
        return four_groups(probe, tables, arrived)[None]
    finished = []
    for j in range(count):
        wave = chain(groups, probe, tables, arrived[0][j], arrived[1][j], finished if j == count - 1 else [])
        finished.append(wave)
    return wave[None]


def four_groups(probe, tables, arrived):
    even, odd = arrived[0], arrived[1]
    count = len(even)
    own = phase_factors(-1, [b[0] for b in even], [b[0] for b in odd])
    near, waves = [], []
    for j in range(count):
        near += phase_factors(2, [even[j][1]], [odd[j][1]])
        waves.append([*second_group(probe, tables, own[j], near[j])])
        waves[j].append(sent_on(waves[j][1], (0, 1), [(0, 2), (1, 3)]))
    finished = []
    for j in range(count):
        wave = last_groups(tables, own[j], near[j], waves[j], finished if j == count - 1 else [])
        finished.append(wave)
    return wave


def solution(mesh):
    return jax.shard_map(
        body,
        mesh=mesh,
        in_specs=(P(), P("depth", "probe", None), P("probe"), P("probe")),
        out_specs=P("depth", "probe", None, None, None),
        check_vma=False,
    )
```

```python
import functools
import math

import numpy as np
import jax
import jax.numpy as jnp
from jax import lax
from jax.experimental import pallas as pl
from jax.experimental.pallas import tpu as pltpu
from jax.sharding import PartitionSpec as P


CHIRP = 40.0
F32 = jnp.float32
BF16 = jnp.bfloat16
OCTAVES = 120.0
ROOM = 8 * 2**20


def handed_down(block, parity):
    strips = lax.axis_size("probe")
    return lax.ppermute(block, "probe", [(i + 1, i) for i in range(parity, strips - 1, 2)])


def sent_on(block, parities, pairs):
    strips = lax.axis_size("probe")
    route = [(a * strips + p, b * strips + p) for a, b in pairs for p in range(strips) if p % 2 in parities]
    return lax.ppermute(block, ("depth", "probe"), route)


def operator_tables(size):
    k = np.arange(size)
    freq = np.where(k < size // 2, k, k - size) / size
    taps = np.fft.ifft(np.exp(-1j * CHIRP * freq * freq))
    half = size // 2
    lag = (np.arange(half)[:, None] - np.arange(half)[None, :]) % size
    right, left = [], []
    for sign in (1.0, -1.0):
        part = 0.5 * (taps[lag] + sign * taps[(lag + half) % size])
        full = np.block([[part.real, part.imag], [-part.imag, part.real]]).astype(np.float32)
        high = full.astype(BF16)
        low = (full - high.astype(np.float32)).astype(BF16)
        right.append(np.concatenate([high, low], axis=0))
        left.append(np.concatenate([high.T, low.T], axis=1))
    return [jnp.asarray(np.stack(right)), jnp.asarray(np.stack(left))]


def fit(function, powers, reach):
    x = np.cos(np.pi * (np.arange(400) + 0.5) / 400) * reach
    basis = np.stack([(x / reach) ** p for p in powers], axis=1)
    found = np.linalg.lstsq(basis, function(x), rcond=None)[0]
    return [float(c / reach**p) for c, p in zip(found, powers)]


REACH = 0.5 * OCTAVES * math.log(2.0)


def half_angle(position):
    return position * (0.5 * math.pi / REACH)


SIN_FIT = fit(lambda y: math.sqrt(2.0) * np.sin(half_angle(y)), (1, 3, 5, 7), REACH)
COS_FIT = fit(lambda y: math.sqrt(2.0) * np.cos(half_angle(y)), (0, 2, 4, 6), REACH)


def horner(square, coefficients):
    value = coefficients[-1]
    for c in coefficients[-2::-1]:
        value = value * square + c
    return value


def phase_factor(code):
    position = jnp.log(code)
    square = position * position
    sine = position * horner(square, SIN_FIT)
    cosine = horner(square, COS_FIT)
    return 1.0 - sine * sine, sine * cosine


def coded(phase):
    turns = phase * (0.5 / math.pi)
    return jnp.exp2(OCTAVES * (turns - jnp.round(turns))).astype(BF16)


SMEM = pl.BlockSpec(memory_space=pltpu.SMEM)
VMEM = pl.BlockSpec(memory_space=pltpu.VMEM)


def product(a, b):
    return jnp.dot(a, b, preferred_element_type=F32)


def propagated(real, imag, right_ref, left_ref):
    size = real.shape[-1]
    half = size // 2

    def right(k, combine):
        data = jnp.concatenate([combine(real[:, :half], real[:, half:]), combine(imag[:, :half], imag[:, half:])], axis=1).astype(BF16)
        return product(data, right_ref[k, :size]) + product(data, right_ref[k, size:])

    plus, minus = right(0, jnp.add), right(1, jnp.subtract)
    re = jnp.concatenate([plus[:, :half], minus[:, :half]], axis=1)
    im = jnp.concatenate([plus[:, half:], minus[:, half:]], axis=1)

    def left(k, combine):
        data = jnp.concatenate([combine(re[:half], re[half:]), combine(im[:half], im[half:])], axis=0).astype(BF16)
        return product(left_ref[k, :, :size], data) + product(left_ref[k, :, size:], data)

    top, low = left(0, jnp.add), left(1, jnp.subtract)
    re = jnp.concatenate([top[:half] + low[:half], top[:half] - low[:half]], axis=0)
    im = jnp.concatenate([top[half:] + low[half:], top[half:] - low[half:]], axis=0)
    real = jnp.concatenate([re[:, :half] + re[:, half:], re[:, :half] - re[:, half:]], axis=1)
    imag = jnp.concatenate([im[:, :half] + im[:, half:], im[:, :half] - im[:, half:]], axis=1)
    return real, imag


def transmitted(real, imag, cosine, sine, right_ref, left_ref):
    real, imag = cosine * real - sine * imag, cosine * imag + sine * real
    return propagated(real, imag, right_ref, left_ref)


def sliced(real, imag, code, right_ref, left_ref):
    return transmitted(real, imag, *phase_factor(code.astype(F32)), right_ref, left_ref)


def window_kernel(count, parity, starts_ref, own_ref, next_ref, *refs):
    outs, scratch = refs[-1 - count : -1], refs[-1]
    layers, strip, width = own_ref.shape
    size = outs[0].shape[-1]
    span = size + 128
    place = lax.axis_index("probe")

    @pl.when(place % 2 == parity)
    def _():
        edge = (place == lax.axis_size("probe") - 1).astype(F32)
        line = lax.broadcasted_iota(jnp.int32, (strip, span), 0)
        for j, out in enumerate(outs):
            r = jnp.max(starts_ref[j, 0]).astype(jnp.int32)
            c = jnp.max(starts_ref[j, 1]).astype(jnp.int32)
            base = jnp.minimum(c // 128, (width - span) // 128)
            shift = c - base * 128
            lanes = pl.ds(pl.multiple_of(base * 128, 128), span)
            for s in range(layers):
                own = own_ref[s, :, lanes].astype(F32)
                following = next_ref[s, :, lanes].astype(F32) + edge
                merged = jnp.where(line >= r, own, following)
                turned = pltpu.roll(merged, span - shift, 1)[:, :size]
                for part in range(size // 128):
                    columns = turned[:, part * 128 : (part + 1) * 128]
                    scratch[part, pl.ds(0, strip), :] = columns
                    scratch[part, pl.ds(strip, strip), :] = columns
                    out[s, :, part * 128 : (part + 1) * 128] = scratch[part, pl.ds(r, size), :].astype(BF16)


def windows(parity, size, starts, own, following, after):
    layers, strip, _ = own.shape
    count = starts.shape[0]
    return pl.pallas_call(
        functools.partial(window_kernel, count, parity),
        out_shape=[jax.ShapeDtypeStruct((layers, size, size), BF16)] * count,
        in_specs=[VMEM] * (3 + len(after)),
        out_specs=[VMEM] * count,
        scratch_shapes=[pltpu.VMEM((size // 128, 2 * strip, 128), F32)],
        compiler_params=pltpu.CompilerParams(vmem_limit_bytes=ROOM),
    )(starts, own, following, *after)


def rounded(state_ref, real, imag):
    state_ref[0] = real.astype(BF16).astype(F32)
    state_ref[1] = imag.astype(BF16).astype(F32)


def chain_kernel(groups, before, probe_ref, right_ref, left_ref, *refs):
    arrived = (refs[:groups], refs[groups : 2 * groups])
    out_ref, state_ref = refs[-2], refs[-1]
    group = lax.axis_index("depth")
    even = lax.axis_index("probe") % 2 == 0

    def block(g, s):
        value = None
        for m in sorted({g ^ own for own in range(g, groups)}):
            this = jnp.where(even, arrived[0][m][s], arrived[1][m][s])
            value = this if value is None else jnp.where(group ^ g == m, this, value)
        return value

    state_ref[...] = probe_ref[...]
    for g in range(groups):

        @pl.when(g <= group)
        def _():
            real, imag = state_ref[0], state_ref[1]
            for s in range(arrived[0][0].shape[0]):
                real, imag = sliced(real, imag, block(g, s), right_ref, left_ref)
            rounded(state_ref, real, imag)

    out_ref[before] = state_ref[...].astype(BF16)
    for j in range(before):
        out_ref[j] = refs[2 * groups + j][0]


def chain(groups, probe, tables, even, odd, finished):
    blocks = [each[m] for each in (even, odd) for m in range(groups)]
    arguments = [probe, *tables, *blocks, *finished]
    return pl.pallas_call(
        functools.partial(chain_kernel, groups, len(finished)),
        out_shape=jax.ShapeDtypeStruct((len(finished) + 1, *probe.shape), BF16),
        in_specs=[VMEM] * len(arguments),
        out_specs=VMEM,
        scratch_shapes=[pltpu.VMEM(probe.shape, F32)],
        compiler_params=pltpu.CompilerParams(vmem_limit_bytes=ROOM),
    )(*arguments)


def factor_kernel(count, unused, *refs):
    even_refs, odd_refs, outs = refs[:count], refs[count : 2 * count], refs[2 * count :]
    even = lax.axis_index("probe") % 2 == 0
    group = lax.axis_index("depth")

    @pl.when(group != unused)
    def _():
        for j in range(count):
            for s in range(even_refs[j].shape[0]):
                code = jnp.where(even, even_refs[j][s], odd_refs[j][s])
                outs[j][s, 0], outs[j][s, 1] = phase_factor(code.astype(F32))


def phase_factors(unused, even, odd):
    count = len(even)
    layers, size, _ = even[0].shape
    return pl.pallas_call(
        functools.partial(factor_kernel, count, unused),
        out_shape=[jax.ShapeDtypeStruct((layers, 2, size, size), F32)] * count,
        in_specs=[VMEM] * (2 * count),
        out_specs=[VMEM] * count,
        compiler_params=pltpu.CompilerParams(vmem_limit_bytes=ROOM),
    )(*even, *odd)


def group_of(state_ref, factor, layers, right_ref, left_ref):
    real, imag = state_ref[0], state_ref[1]
    for s in range(layers):
        real, imag = transmitted(real, imag, factor(s, 0), factor(s, 1), right_ref, left_ref)
    rounded(state_ref, real, imag)


def second_kernel(probe_ref, right_ref, left_ref, own_ref, near_ref, first_ref, second_ref, state_ref):
    group = lax.axis_index("depth")

    @pl.when(group < 2)
    def _():
        state_ref[...] = probe_ref[...]
        for g, out_ref in enumerate((first_ref, second_ref)):
            factor = lambda s, k: jnp.where(group == g, own_ref[s, k], near_ref[s, k])
            group_of(state_ref, factor, own_ref.shape[0], right_ref, left_ref)
            out_ref[...] = state_ref[...].astype(BF16)


def second_group(probe, tables, own, near):
    return pl.pallas_call(
        second_kernel,
        out_shape=[jax.ShapeDtypeStruct(probe.shape, BF16)] * 2,
        in_specs=[VMEM] * 5,
        out_specs=[VMEM] * 2,
        scratch_shapes=[pltpu.VMEM(probe.shape, F32)],
        compiler_params=pltpu.CompilerParams(vmem_limit_bytes=ROOM),
    )(probe, *tables, own, near)


def last_kernel(before, right_ref, left_ref, own_ref, near_ref, first_ref, second_ref, far_ref, *refs):
    finished = refs[:before]
    out_ref, state_ref = refs[before : before + 2]
    copies = []
    if before:
        wave_ref, done = refs[before + 2 :]
        copies = [pltpu.make_async_copy(ref.at[0], out_ref.at[j], done.at[j]) for j, ref in enumerate(finished)]
    for copy in copies:
        copy.start()
    layers = own_ref.shape[0]
    group = lax.axis_index("depth")
    for part in range(2):
        value = jnp.where(group == 0, first_ref[part], second_ref[part])
        value = jnp.where(group >= 2, far_ref[part], value)
        state_ref[part] = value.astype(F32)

    @pl.when(group == 3)
    def _():
        group_of(state_ref, lambda s, k: near_ref[s, k], layers, right_ref, left_ref)

    @pl.when(group >= 2)
    def _():
        group_of(state_ref, lambda s, k: own_ref[s, k], layers, right_ref, left_ref)

    if before:
        wave_ref[...] = state_ref[...].astype(BF16)
        copies.append(pltpu.make_async_copy(wave_ref, out_ref.at[before], done.at[before]))
        copies[-1].start()
    else:
        out_ref[0] = state_ref[...].astype(BF16)
    for copy in copies:
        copy.wait()


def last_groups(tables, own, near, waves, finished):
    shape = waves[0].shape
    before = len(finished)
    scratch = [pltpu.VMEM(shape, F32)]
    if before:
        scratch += [pltpu.VMEM(shape, BF16), pltpu.SemaphoreType.DMA((before + 1,))]
    arguments = [*tables, own, near, *waves, *finished]
    return pl.pallas_call(
        functools.partial(last_kernel, before),
        out_shape=jax.ShapeDtypeStruct((len(finished) + 1, *shape), BF16),
        in_specs=[VMEM] * len(arguments),
        out_specs=pl.BlockSpec(memory_space=pl.ANY) if before else VMEM,
        scratch_shapes=scratch,
        compiler_params=pltpu.CompilerParams(vmem_limit_bytes=ROOM),
    )(*arguments)


def mark_kernel(block_ref, out_ref):
    out_ref[...] = block_ref[0, :16, :128]


def mark(block):
    return pl.pallas_call(
        mark_kernel,
        out_shape=jax.ShapeDtypeStruct((16, 128), BF16),
        in_specs=[VMEM],
        out_specs=VMEM,
        compiler_params=pltpu.CompilerParams(vmem_limit_bytes=ROOM),
    )(block)


def pairs_at(groups, m):
    if groups == 4:
        return [(0, 1), (1, 0), (2, 3)]
    return [(i, i ^ m) for i in range(groups) if i < i ^ m < groups]


def hops(groups, count):
    return [(j, m) for j in range(count) for m in range(1, 2 if groups == 4 else groups)]


def body(probe, phase, row_offsets, col_offsets):
    size = probe.shape[-1]
    strip = phase.shape[1]
    count = row_offsets.shape[0]
    groups = lax.axis_size("depth")
    starts = jnp.stack([row_offsets - lax.axis_index("probe") * strip, col_offsets], axis=1)
    starts = jnp.broadcast_to(starts.astype(F32)[:, :, None, None], (count, 2, 8, 128))
    tables = operator_tables(size)
    own = coded(phase)
    following = {}
    for parity in (1, 0):
        following[parity] = handed_down(own, parity)
    arrived = {}
    after = []
    for parity in (0, 1):
        firsts = windows(parity, size, starts, own, following[parity], after)
        blocks = [{0: first} for first in firsts]
        for j, m in hops(groups, count):
            blocks[j][m] = sent_on(firsts[j], (parity,), pairs_at(groups, m))
        if parity == 0:
            after = [mark(firsts[-1])]
        arrived[parity] = blocks
    if groups == 4:
        return four_groups(probe, tables, arrived)[None]
    finished = []
    for j in range(count):
        wave = chain(groups, probe, tables, arrived[0][j], arrived[1][j], finished if j == count - 1 else [])
        finished.append(wave)
    return wave[None]


def four_groups(probe, tables, arrived):
    even, odd = arrived[0], arrived[1]
    count = len(even)
    own = phase_factors(-1, [b[0] for b in even], [b[0] for b in odd])
    near, waves = [], []
    for j in range(count):
        near += phase_factors(2, [even[j][1]], [odd[j][1]])
        waves.append([*second_group(probe, tables, own[j], near[j])])
        waves[j].append(sent_on(waves[j][1], (0, 1), [(0, 2), (1, 3)]))
    finished = []
    for j in range(count):
        wave = last_groups(tables, own[j], near[j], waves[j], finished if j == count - 1 else [])
        finished.append(wave)
    return wave


def solution(mesh):
    return jax.shard_map(
        body,
        mesh=mesh,
        in_specs=(P(), P("depth", "probe", None), P("probe"), P("probe")),
        out_specs=P("depth", "probe", None, None, None),
        check_vma=False,
    )
```
